32 devices in a mesh: row: 4 (over x, core), col: 8 (over z, y).
Axes of the slice: x: 2, y: 2, z: 4, core: 2. Of those that a mesh axis runs over, the one named last changes fastest.
Arguments:
- trailing: float32 [4096, 4096], P('row', 'col'), may hold values from -6 to 6
- panel_left: float32 [4096, 384], P(('row', 'col')), may hold values from -0.3125 to 0.3125
- panel_right: float32 [8, 1024, 384], P('row', 'col'), may hold values from -1 to 1
- panel_solved: float32 [1024, 1024], P('row', 'col'), may hold values from -1.75 to 1.75
- right_sides: float32 [4096, 1024], P('row', 'col'), may hold values from -6 to 6
- tile_ranks: int32 [8], replicated, may hold values from 64 to 384, as said below
- tile_order: int32 [8], replicated, may hold values from 0 to 7, each once
Outputs:
- trail_new: float32 [4096, 4096], P('row', 'col')
- rhs_new: float32 [4096, 1024], P('row', 'col')
The draws below stay inside these ranges and needn't reach their ends.
Inputs may be any that keep to these rules, and one draw needn't show every extreme that they name: `tile_ranks`: every rank is a multiple of 64; both 64 and 384 occur in every draw. `tile_order`: each tile appears in exactly one slot.
All inputs are finite; a program needn't handle non-finite values.
Results may differ from the reference program's by a relative error of at most 0.00008.
Values sent between devices are 32-bit elements; how exact they have to be, the bound alone decides.
A program may use at most 64 MiB of HBM per device.

```python
import jax
import jax.numpy as jnp
from jax import lax

TILE = 512
PANEL = 1024
RSTEP = 64
RMAX = 384
TILES = 8
ORDER = 4096
RHS_COLS = 1024


def draw_tile_ranks(key, part):
    first_key, second_key = jax.random.split(jax.random.fold_in(key, 17))
    levels = jax.random.randint(first_key, (TILES,), 1, 7)
    spots = jax.random.permutation(second_key, TILES)
    places = jnp.arange(TILES)
    levels = jnp.where(places == spots[0], 6, levels)
    levels = jnp.where(places == spots[1], 1, levels)
    return (levels * RSTEP).astype(jnp.int32)


def level_of(key, extent, cuts, least, high):
    loudness = 1.0
    for position, shards_of in cuts:
        draws = jax.random.uniform(jax.random.fold_in(jax.random.fold_in(key, 6), position), (shards_of,), jnp.float32, least / len(cuts), high / len(cuts))
        loudness = loudness * jnp.repeat(jnp.exp(draws), extent[position] // shards_of).reshape((-1,) + (1,) * (len(extent) - 1 - position))
    return loudness


def gaussian(rng, shape, spread, limit, cuts=(), kind=jnp.bfloat16):
    array = jax.random.normal(rng, shape, jnp.float32) * spread
    if len(cuts) > 0:
        array = level_of(rng, shape, cuts, -0.22, 0.18) * array
    return jnp.clip(array, min=-limit, max=limit).astype(kind)


def setup_inputs(seed: int = 0) -> dict:
    key_list = jax.random.split(jax.random.key(seed), 8)
    trailing = gaussian(key_list[0], (ORDER, ORDER), 1.0, 6.0, ((0, 4), (1, 8)), jnp.float32)
    panel_left = gaussian(key_list[1], (ORDER, RMAX), RMAX ** -0.5, 0.3125, ((0, 32),), jnp.float32)
    panel_right = gaussian(key_list[2], (TILES, PANEL, RMAX), (PANEL ** -0.25), 1.0, ((0, 4), (1, 8)), jnp.float32)
    panel_solved = gaussian(key_list[3], (PANEL, RHS_COLS), 0.3, 1.75, ((0, 4), (1, 8)), jnp.float32)
    right_sides = gaussian(key_list[4], (ORDER, RHS_COLS), 1.0, 6.0, ((0, 4), (1, 8)), jnp.float32)
    tile_ranks = draw_tile_ranks(jax.random.fold_in(key_list[7], 71), 0)
    tile_order = jax.random.permutation(key_list[6], TILES).astype(jnp.int32)
    return {"trailing": trailing, "panel_left": panel_left, "panel_right": panel_right, "panel_solved": panel_solved, "right_sides": right_sides, "tile_ranks": tile_ranks, "tile_order": tile_order}


def reference(trailing, panel_left, panel_right, panel_solved, right_sides, tile_ranks, tile_order):
    places = jnp.arange(TILES, dtype=jnp.int32)
    slot_rank = jnp.take(tile_ranks, tile_order)
    keep_mask = (jnp.arange(RMAX, dtype=jnp.int32)[None, :] < slot_rank[:, None]).astype(jnp.float32)
    left_factor = panel_left.reshape(TILES, TILE, RMAX) * keep_mask[:, None, :]
    panel_l = jnp.einsum("sik,sjk->sij", left_factor, panel_right, precision=lax.Precision.HIGHEST).reshape(TILES * TILE, PANEL)
    slot_of = jnp.zeros((TILES,), jnp.int32).at[tile_order].set(places)
    column_l = jnp.take(panel_l.reshape(TILES, TILE, PANEL), slot_of, axis=0).reshape(TILES * TILE, PANEL)
    trail_new = trailing - jnp.dot(panel_l, column_l.T, precision=lax.Precision.HIGHEST, preferred_element_type=jnp.float32)
    rhs_new = right_sides - jnp.dot(panel_l, panel_solved, precision=lax.Precision.HIGHEST, preferred_element_type=jnp.float32)
    return trail_new, rhs_new
```

```python
import functools

import jax
import jax.numpy as jnp
from jax import lax
from jax.experimental import pallas as pl
from jax.experimental.pallas import tpu as pltpu
from jax.sharding import PartitionSpec as P

MESH = pl.DeviceIdType.MESH
ACROSS = 2
CORES = 2


def gather_kernel(n_row, n_col, slots, place, left, right, solved, rows_l, rows_r, tile, rows_w,
                  first_out, first_in, chip, far_in, own_sem, rsem, zsem, ysem, fsem, frsem, xsem, xrsem, tsem, trsem, wsem, wrsem):
    length = n_col // ACROSS
    half = length // slots
    teams = n_row // CORES
    row, col = lax.axis_index("row"), lax.axis_index("col")
    z, y = col // ACROSS, col % ACROSS
    team, core = row // CORES, row % CORES
    pair = team * CORES + (1 - core)
    mate = z * ACROSS + (1 - y)

    barrier = pltpu.get_barrier_semaphore()

    def greet(r, c):
        pl.semaphore_signal(barrier, inc=1, device_id=(r, c), device_id_type=MESH)

    @pl.when(z > 0)
    def _():
        greet(row, col - ACROSS)

    @pl.when(z < length - 1)
    def _():
        greet(row, col + ACROSS)

    greet(row, mate)
    for k in range(1, n_row):
        greet(lax.rem(row + k, n_row), col)

    def piece(p, c):
        return rows_l.at[c] if p == 0 else rows_r.at[p - 1, c]

    own = [pltpu.make_async_copy(left, piece(0, col), own_sem.at[0])]
    for s in range(slots):
        own.append(pltpu.make_async_copy(right.at[s], piece(s + 1, col), own_sem.at[s + 1]))
    own.append(pltpu.make_async_copy(solved, rows_w.at[row], own_sem.at[slots + 1]))
    for copy in own:
        copy.start()
    for copy in own:
        copy.wait()
    pl.semaphore_wait(barrier, (z > 0).astype(jnp.int32) + (z < length - 1).astype(jnp.int32) + n_row)

    def z_copy(p, src, way):
        c = src * ACROSS + y
        to = col + (ACROSS if way == 0 else -ACROSS)
        return pltpu.make_async_remote_copy(piece(p, c), piece(p, c), zsem.at[way, p, src], rsem.at[p, c], device_id=(row, to), device_id_type=MESH)

    def y_copy(p, src, c):
        return pltpu.make_async_remote_copy(piece(p, c), piece(p, c), ysem.at[p, src], rsem.at[p, c], device_id=(row, mate), device_id_type=MESH)

    def w_copy(k):
        return pltpu.make_async_remote_copy(rows_w.at[row], rows_w.at[row], wsem.at[k], wrsem.at[row], device_id=(lax.rem(row + k, n_row), col), device_id_type=MESH)

    def f_copy(i):
        return pltpu.make_async_remote_copy(first_out.at[i], first_in.at[i], fsem.at[i], frsem.at[i], device_id=(pair, col), device_id_type=MESH)

    def x_copy(i, k, source):
        to = lax.rem(team + k, teams)
        return pltpu.make_async_remote_copy(chip.at[i], far_in.at[source, i], xsem.at[k, i], xrsem.at[source, i], device_id=(to * CORES + core, col), device_id_type=MESH)

    def t_copy(i, c):
        return pltpu.make_async_remote_copy(tile.at[c], tile.at[c], tsem.at[i], trsem.at[c], device_id=(pair, col), device_id_type=MESH)

    for k in range(1, n_row):
        w_copy(k).start()

    root_slot = place[0]
    local = lax.rem(root_slot, slots)
    root_row = root_slot // slots
    root_team = root_row // CORES

    def candidate(i, which, is_left):
        parts = []
        for s in range(slots):
            if is_left:
                parts.append(rows_l[((i - length) + s * half) * ACROSS + which])
            else:
                parts.append(rows_r[s, i * ACROSS + which])
        value = parts[0]
        for s in range(1, slots):
            value = jnp.where(local == s, parts[s], value)
        return value

    def stage_one(i, is_left):
        first_out[i] = candidate(i, 1 - core, is_left)
        f_copy(i).start()

    def stage_two(i, is_left):
        mine = candidate(i, core, is_left)
        f_copy(i).wait_recv()
        chip[i] = jnp.where(root_row == row, mine, first_in[i])
        for k in range(1, teams):
            x_copy(i, k, team).start()

    def stage_three(i, is_left):
        value = chip[i]
        for k in range(1, teams):
            other = lax.rem(team + k, teams)
            x_copy(i, k, other).wait_recv()
            value = jnp.where(root_team == other, far_in[other, i], value)
        c = i * ACROSS + core
        tile[c] = value
        t_copy(i, c).start()

    def sources(d, body):
        for side in range(2):
            src = z - d if side == 0 else z + d
            ok = src >= 0 if side == 0 else (src < length) & (d > 0)
            pl.when(ok)(functools.partial(body, src, side))

    def ready(d, body):
        def lefts(q, _):
            last = jnp.maximum(jnp.abs(z - q), jnp.abs(z - q - half))
            for s in range(1, slots):
                last = jnp.maximum(last, jnp.abs(z - q - s * half))

            @pl.when(last == d)
            def _():
                body(length + q, True)

            return 0

        lax.fori_loop(0, half, lefts, 0)
        sources(d, lambda src, side: body(src, False))

    def forward(d):
        for p in range(slots + 1):
            def one(src, side, p=p):
                @pl.when(d > 0)
                def _():
                    y_copy(p, src, src * ACROSS + y).wait_recv()

                @pl.when((z < length - 1) & ((side == 0) | (d == 0)))
                def _():
                    z_copy(p, src, 0).start()

                @pl.when((z > 0) & ((side == 1) | (d == 0)))
                def _():
                    z_copy(p, src, 1).start()

                y_copy(p, src, src * ACROSS + y).start()

            sources(d, one)

    def arrive(d):
        def one(src, side):
            for p in range(slots + 1):
                y_copy(p, src, src * ACROSS + 1 - y).wait_recv()

        sources(d, one)

    def step(d, _):
        @pl.when(d < length)
        def _():
            forward(d)

        @pl.when((d >= 1) & (d <= length))
        def _():
            arrive(d - 1)
            ready(d - 1, stage_one)
            ready(d - 1, stage_two)

        @pl.when(d >= 2)
        def _():
            ready(d - 2, stage_three)

        return 0

    lax.fori_loop(0, length + 2, step, 0)

    def drain(d, _):
        for p in range(slots + 1):
            def one(src, side, p=p):
                @pl.when((z < length - 1) & ((side == 0) | (d == 0)))
                def _():
                    z_copy(p, src, 0).wait_send()

                @pl.when((z > 0) & ((side == 1) | (d == 0)))
                def _():
                    z_copy(p, src, 1).wait_send()

                y_copy(p, src, src * ACROSS + y).wait_send()

            sources(d, one)
        return 0

    lax.fori_loop(0, length, drain, 0)

    def finish(i, _):
        f_copy(i).wait_send()
        for k in range(1, teams):
            x_copy(i, k, team).wait_send()
        t_copy(i, i * ACROSS + core).wait_send()
        t_copy(i, i * ACROSS + 1 - core).wait_recv()
        return 0

    lax.fori_loop(0, length + half, finish, 0)
    for k in range(1, n_row):
        w_copy(k).wait_send()
        other = lax.rem(row + k, n_row)
        pltpu.make_async_remote_copy(rows_w.at[other], rows_w.at[other], wsem.at[k], wrsem.at[other], device_id=(other, col), device_id_type=MESH).wait_recv()


def gather(n_row, n_col, place, left, right, solved):
    slots, depth, width = right.shape
    length = n_col // ACROSS
    half = length // slots
    teams = n_row // CORES
    chunks = length + half
    f32 = jnp.float32
    block = (depth, width)
    vmem = pl.BlockSpec(memory_space=pltpu.VMEM)
    dma = pltpu.SemaphoreType.DMA
    return pl.pallas_call(
        functools.partial(gather_kernel, n_row, n_col, slots),
        out_shape=(
            jax.ShapeDtypeStruct((n_col,) + left.shape, f32),
            jax.ShapeDtypeStruct((slots, n_col) + block, f32),
            jax.ShapeDtypeStruct((chunks * ACROSS,) + block, f32),
            jax.ShapeDtypeStruct((n_row,) + solved.shape, f32),
        ),
        in_specs=[pl.BlockSpec(memory_space=pltpu.SMEM), vmem, vmem, vmem],
        out_specs=(vmem, vmem, vmem, vmem),
        scratch_shapes=[
            pltpu.VMEM((chunks,) + block, f32),
            pltpu.VMEM((chunks,) + block, f32),
            pltpu.VMEM((chunks,) + block, f32),
            pltpu.VMEM((teams, chunks) + block, f32),
            dma((slots + 2,)),
            dma((slots + 1, n_col)),
            dma((2, slots + 1, length)),
            dma((slots + 1, length)),
            dma((chunks,)),
            dma((chunks,)),
            dma((teams, chunks)),
            dma((teams, chunks)),
            dma((chunks,)),
            dma((chunks * ACROSS,)),
            dma((n_row,)),
            dma((n_row,)),
        ],
        compiler_params=pltpu.CompilerParams(collective_id=0, has_side_effects=True, vmem_limit_bytes=48 * 1024 * 1024),
        name="gather_panel",
    )(place, left, right, solved)


def high(spec, a, b):
    return jnp.einsum(spec, a, b, precision=lax.Precision.HIGH, preferred_element_type=jnp.float32)


def on_device(n_row, n_col, trailing, panel_left, panel_right, panel_solved, right_sides, tile_ranks, tile_order):
    slots, _, width = panel_right.shape
    count = tile_order.shape[0]
    row, column = lax.axis_index("row"), lax.axis_index("col")
    places = jnp.arange(count, dtype=jnp.int32)
    levels = jnp.arange(width, dtype=jnp.int32)
    root = jnp.sum(jnp.where(tile_order == column, places, 0)).astype(jnp.int32)
    rows_l, rows_r, tile, rows_w = gather(n_row, n_col, root[None], panel_left, panel_right, panel_solved)
    slot_ids = row * slots + jnp.arange(slots, dtype=jnp.int32)
    my_tiles = jnp.sum(jnp.where(places[None, :] == slot_ids[:, None], tile_order[None, :], 0), axis=1)
    my_ranks = jnp.sum(jnp.where(places[None, :] == my_tiles[:, None], tile_ranks[None, :], 0), axis=1)
    column_rank = jnp.sum(jnp.where(places == column, tile_ranks, 0))
    left = rows_l.reshape(slots, -1, width)
    left = jnp.where(levels[None, None, :] < my_ranks[:, None, None], left, 0.0)
    right = rows_r.reshape(slots, -1, width)
    tile_right = tile[:n_col].reshape(-1, width)
    tile_left = tile[n_col:].reshape(-1, width)
    tile_left = jnp.where(levels[None, :] < column_rank, tile_left, 0.0)
    solved = rows_w.reshape(-1, rows_w.shape[-1])
    both = high("sjk,jm->skm", right, jnp.concatenate([tile_right, solved], 1))
    middle = high("skm,im->ski", both[:, :, :width], tile_left)
    update = high("sik,skn->sin", left, jnp.concatenate([middle, both[:, :, width:]], 2))
    tile_rows = tile_left.shape[0]
    update = update.reshape(slots * tile_rows, -1)
    return trailing - update[:, :tile_rows], right_sides - update[:, tile_rows:]


def solution(mesh):
    return jax.shard_map(
        functools.partial(on_device, mesh.shape["row"], mesh.shape["col"]),
        mesh=mesh,
        in_specs=(
            P("row", "col"),
            P(("row", "col"), None),
            P("row", "col", None),
            P("row", "col"),
            P("row", "col"),
            P(),
            P(),
        ),
        out_specs=(P("row", "col"), P("row", "col")),
        check_vma=False,
    )
```

```python
import functools

import jax
import jax.numpy as jnp
from jax import lax
from jax.experimental import pallas as pl
from jax.experimental.pallas import tpu as pltpu
from jax.sharding import PartitionSpec as P

MESH = pl.DeviceIdType.MESH
ACROSS = 2
CORES = 2


def sides(z, length, d, body):
    for side in range(2):
        src = z - d if side == 0 else z + d
        ok = src >= 0 if side == 0 else (src < length) & (d > 0)
        pl.when(ok)(functools.partial(body, src, side))


def find(order, value):
    place = jnp.int32(0)
    for i in range(order.shape[0]):
        place = jnp.where(order[i] == value, jnp.int32(i), place)
    return place


def gather_kernel(n_row, n_col, slots, order, left, right, solved, rows_l, rows_r, tile, rows_w,
                  first_out, first_in, chip, far_in, own_sem, rsem, zsem, ysem, fsem, frsem, xsem, xrsem, tsem, trsem, wsem, wrsem):
    length = n_col // ACROSS
    half = length // slots
    teams = n_row // CORES
    part = tile.shape[1] // CORES
    late = slots + 1
    row, col = lax.axis_index("row"), lax.axis_index("col")
    z, y = col // ACROSS, col % ACROSS
    team, core = row // CORES, row % CORES
    pair = team * CORES + (1 - core)
    mate = z * ACROSS + (1 - y)

    barrier = pltpu.get_barrier_semaphore()

    def greet(r, c):
        pl.semaphore_signal(barrier, inc=1, device_id=(r, c), device_id_type=MESH)

    @pl.when(z > 0)
    def _():
        greet(row, col - ACROSS)

    @pl.when(z < length - 1)
    def _():
        greet(row, col + ACROSS)

    greet(row, mate)
    for k in range(1, n_row):
        greet(lax.rem(row + k, n_row), col)

    cut = left.shape[0] // 2

    def piece(p, c):
        if p == 0:
            return rows_l.at[c, pl.ds(0, cut)]
        if p == late:
            return rows_l.at[c, pl.ds(cut, cut)]
        return rows_r.at[p - 1, c]

    own = [pltpu.make_async_copy(left, rows_l.at[col], own_sem.at[0])]
    for s in range(slots):
        own.append(pltpu.make_async_copy(right.at[s], piece(s + 1, col), own_sem.at[s + 1]))
    own.append(pltpu.make_async_copy(solved, rows_w.at[row], own_sem.at[slots + 1]))
    for copy in own:
        copy.start()
    for copy in own:
        copy.wait()
    pl.semaphore_wait(barrier, (z > 0).astype(jnp.int32) + (z < length - 1).astype(jnp.int32) + n_row)

    def z_copy(p, src, way, across=None):
        c = src * ACROSS + (y if across is None else across)
        lane = p if across is None else late + 1
        to = col + (ACROSS if way == 0 else -ACROSS)
        return pltpu.make_async_remote_copy(piece(p, c), piece(p, c), zsem.at[way, lane, src], rsem.at[p, c], device_id=(row, to), device_id_type=MESH)

    def y_copy(p, src, c):
        return pltpu.make_async_remote_copy(piece(p, c), piece(p, c), ysem.at[p, src], rsem.at[p, c], device_id=(row, mate), device_id_type=MESH)

    def w_copy(k):
        return pltpu.make_async_remote_copy(rows_w.at[row], rows_w.at[row], wsem.at[k], wrsem.at[row], device_id=(lax.rem(row + k, n_row), col), device_id_type=MESH)

    def f_copy(c):
        return pltpu.make_async_remote_copy(first_out.at[c], first_in.at[c], fsem.at[c], frsem.at[c], device_id=(pair, col), device_id_type=MESH)

    def x_copy(c, k, source):
        to = lax.rem(team + k, teams)
        return pltpu.make_async_remote_copy(chip.at[c], far_in.at[source, c], xsem.at[k, c], xrsem.at[source, c], device_id=(to * CORES + core, col), device_id_type=MESH)

    def rows_of(which):
        return pl.ds(pl.multiple_of(which * part, part), part)

    def t_copy(c, which):
        ref = tile.at[c, rows_of(which)]
        return pltpu.make_async_remote_copy(ref, ref, tsem.at[c], trsem.at[c], device_id=(pair, col), device_id_type=MESH)

    root_slot = find(order, col)
    local = lax.rem(root_slot, slots)
    root_row = root_slot // slots
    root_team = root_row // CORES

    def candidate(c, which, is_left):
        parts = []
        for s in range(slots):
            if is_left:
                parts.append(rows_l[(c - n_col) + s * (n_col // slots), rows_of(which)])
            else:
                parts.append(rows_r[s, c, rows_of(which)])
        value = parts[0]
        for s in range(1, slots):
            value = jnp.where(local == s, parts[s], value)
        return value

    def stage_one(c, is_left):
        first_out[c] = candidate(c, 1 - core, is_left)
        f_copy(c).start()

    def stage_two(c, is_left):
        mine = candidate(c, core, is_left)
        f_copy(c).wait_recv()
        chip[c] = jnp.where(root_row == row, mine, first_in[c])
        for k in range(1, teams):
            x_copy(c, k, team).start()

    def stage_three(c, is_left):
        value = chip[c]
        for k in range(1, teams):
            other = lax.rem(team + k, teams)
            x_copy(c, k, other).wait_recv()
            value = jnp.where(root_team == other, far_in[other, c], value)
        tile[c, rows_of(core)] = value
        t_copy(c, core).start()

    def sources(d, body):
        sides(z, length, d, body)

    def near(d, body):
        sources(d, lambda src, side: body(src * ACROSS + y, False))

    def lefts(d, body):
        def one(q, _):
            last = jnp.abs(z - q)
            for s in range(1, slots):
                last = jnp.maximum(last, jnp.abs(z - q - s * half))

            @pl.when(last == d)
            def _():
                for across in range(ACROSS):
                    body(n_col + q * ACROSS + across, True)

            return 0

        lax.fori_loop(0, half, one, 0)

    def far(d, body):
        lefts(d, body)
        sources(d, lambda src, side: body(src * ACROSS + 1 - y, False))

    def along(d, side, act):
        @pl.when((z < length - 1) & ((side == 0) | (d == 0)))
        def _():
            act(0)

        @pl.when((z > 0) & ((side == 1) | (d == 0)))
        def _():
            act(1)

    def forward(d):
        for p in range(late):
            def one(src, side, p=p):
                @pl.when(d > 0)
                def _():
                    y_copy(p, src, src * ACROSS + y).wait_recv()

                y_copy(p, src, src * ACROSS + y).start()
                along(d, side, lambda way: z_copy(p, src, way).start())

            sources(d, one)

        def both(src, side):
            @pl.when(d > 0)
            def _():
                y_copy(late, src, src * ACROSS + y).wait_recv()

            @pl.when(d == 0)
            def _():
                y_copy(late, src, src * ACROSS + y).start()

            along(d, side, lambda way: z_copy(late, src, way).start())
            y_copy(late, src, src * ACROSS + 1 - y).wait_recv()
            along(d, side, lambda way: z_copy(late, src, way, 1 - y).start())

        sources(d, both)

    def arrive(d):
        def one(src, side):
            for p in range(late):
                y_copy(p, src, src * ACROSS + 1 - y).wait_recv()

        sources(d, one)

    def step(d, _):
        @pl.when(d < length)
        def _():
            forward(d)
            near(d, stage_one)

        @pl.when(d == 0)
        def _():
            for k in range(1, n_row):
                w_copy(k).start()

        @pl.when((d >= 1) & (d <= length))
        def _():
            arrive(d - 1)
            far(d - 1, stage_one)

        @pl.when(d < length)
        def _():
            near(d, stage_two)

        @pl.when((d >= 1) & (d <= length))
        def _():
            far(d - 1, stage_two)
            near(d - 1, stage_three)

        @pl.when(d >= 2)
        def _():
            far(d - 2, stage_three)

        return 0

    lax.fori_loop(0, length + 2, step, 0)

    def drain(d, _):
        def one(src, side):
            for p in range(late):
                y_copy(p, src, src * ACROSS + y).wait_send()
                along(d, side, lambda way: z_copy(p, src, way).wait_send())

            @pl.when(d == 0)
            def _():
                y_copy(late, src, src * ACROSS + y).wait_send()

            along(d, side, lambda way: z_copy(late, src, way).wait_send())
            along(d, side, lambda way: z_copy(late, src, way, 1 - y).wait_send())

        sources(d, one)
        return 0

    lax.fori_loop(0, length, drain, 0)

    def finish(c, _):
        f_copy(c).wait_send()
        for k in range(1, teams):
            x_copy(c, k, team).wait_send()
        t_copy(c, core).wait_send()
        t_copy(c, 1 - core).wait_recv()
        return 0

    lax.fori_loop(0, n_col + half * ACROSS, finish, 0)
    for k in range(1, n_row):
        w_copy(k).wait_send()
        other = lax.rem(row + k, n_row)
        pltpu.make_async_remote_copy(rows_w.at[other], rows_w.at[other], wsem.at[k], wrsem.at[other], device_id=(other, col), device_id_type=MESH).wait_recv()


def gather(n_row, n_col, order, left, right, solved):
    slots, depth, width = right.shape
    length = n_col // ACROSS
    teams = n_row // CORES
    chunks = n_col + n_col // slots
    f32 = jnp.float32
    block = (depth, width)
    part = (depth // CORES, width)
    vmem = pl.BlockSpec(memory_space=pltpu.VMEM)
    hbm = pl.BlockSpec(memory_space=pltpu.HBM)
    dma = pltpu.SemaphoreType.DMA
    return pl.pallas_call(
        functools.partial(gather_kernel, n_row, n_col, slots),
        out_shape=(
            jax.ShapeDtypeStruct((n_col,) + left.shape, f32),
            jax.ShapeDtypeStruct((slots, n_col) + block, f32),
            jax.ShapeDtypeStruct((chunks,) + block, f32),
            jax.ShapeDtypeStruct((n_row,) + solved.shape, f32),
        ),
        in_specs=[pl.BlockSpec(memory_space=pltpu.SMEM), hbm, hbm, hbm],
        out_specs=(vmem, vmem, vmem, vmem),
        scratch_shapes=[
            pltpu.VMEM((chunks,) + part, f32),
            pltpu.VMEM((chunks,) + part, f32),
            pltpu.VMEM((chunks,) + part, f32),
            pltpu.VMEM((teams, chunks) + part, f32),
            dma((slots + 2,)),
            dma((slots + 2, n_col)),
            dma((2, slots + 3, length)),
            dma((slots + 2, length)),
            dma((chunks,)),
            dma((chunks,)),
            dma((teams, chunks)),
            dma((teams, chunks)),
            dma((chunks,)),
            dma((chunks,)),
            dma((n_row,)),
            dma((n_row,)),
        ],
        compiler_params=pltpu.CompilerParams(collective_id=0, has_side_effects=True, vmem_limit_bytes=28 * 1024 * 1024),
        name="gather_panel",
    )(order, left, right, solved)


def cut_two(x):
    high = x.astype(jnp.bfloat16)
    return high, (x - high.astype(jnp.float32)).astype(jnp.bfloat16)


def dot3(a, b, dims):
    (ah, al), (bh, bl) = a, b

    def dot(u, v):
        return lax.dot_general(u, v, (dims, ((), ())), preferred_element_type=jnp.float32)

    return dot(ah, bh) + (dot(ah, bl) + dot(al, bh))


def update_kernel(order, ranks, rows_l, rows_r, tile, rows_w, trailing, sides_in, trail_out, rhs_out, mid_high, mid_low):
    slots = rows_r.shape[0]
    n_col, depth, width = tile.shape
    n_col = rows_r.shape[1]
    slot, step = pl.program_id(0), pl.program_id(1)

    @pl.when(step == 0)
    def _():
        tile_id = order[lax.axis_index("row") * slots + slot]
        rank = ranks[tile_id]
        column_rank = ranks[lax.axis_index("col")]
        lane = lax.broadcasted_iota(jnp.int32, (1, width), 1)
        sub = lax.broadcasted_iota(jnp.int32, (width, 1), 0)
        right = cut_two(rows_r[slot].reshape(n_col * depth, width))
        tile_right = cut_two(tile[:n_col].reshape(n_col * depth, width))
        solved = cut_two(rows_w[...].reshape(n_col * depth, rows_w.shape[2]))
        gram = dot3(right, tile_right, ((0,), (0,)))
        tile_left = tile[n_col:].reshape(-1, width)
        tile_left = cut_two(jnp.where(lane < column_rank, tile_left, 0.0))
        middle = dot3(cut_two(gram), tile_left, ((1,), (1,)))
        rhs = dot3(right, solved, ((0,), (0,)))
        middle = jnp.where(sub < rank, middle, 0.0)
        rhs = jnp.where(sub < rank, rhs, 0.0)
        rows = middle.shape[1]
        mid_high[:, :rows], mid_low[:, :rows] = cut_two(middle)
        mid_high[:, rows:], mid_low[:, rows:] = cut_two(rhs)

    left = cut_two(rows_l[0])
    update = dot3(left, (mid_high[...], mid_low[...]), ((1,), (0,)))
    rows = trailing.shape[1]
    trail_out[...] = trailing[...] - update[:, :rows]
    rhs_out[...] = sides_in[...] - update[:, rows:]


def update(order, ranks, rows_l, rows_r, tile, rows_w, trailing, right_sides):
    slots, width = rows_r.shape[0], rows_r.shape[3]
    rows, columns = trailing.shape
    others = right_sides.shape[1]
    blocks = 2
    size = rows // slots // blocks
    rows_l = rows_l.reshape(slots * blocks, size, width)
    smem = pl.BlockSpec(memory_space=pltpu.SMEM)
    vmem = pl.BlockSpec(memory_space=pltpu.VMEM)

    def place(s, i):
        return (s * blocks + i, 0)

    return pl.pallas_call(
        update_kernel,
        grid=(slots, blocks),
        out_shape=(jax.ShapeDtypeStruct(trailing.shape, jnp.float32), jax.ShapeDtypeStruct(right_sides.shape, jnp.float32)),
        in_specs=[
            smem,
            smem,
            pl.BlockSpec((1, size, width), lambda s, i: (s * blocks + i, 0, 0)),
            vmem,
            vmem,
            vmem,
            pl.BlockSpec((size, columns), place),
            pl.BlockSpec((size, others), place),
        ],
        out_specs=(pl.BlockSpec((size, columns), place), pl.BlockSpec((size, others), place)),
        scratch_shapes=[pltpu.VMEM((width, columns + others), jnp.bfloat16)] * 2,
        compiler_params=pltpu.CompilerParams(vmem_limit_bytes=28 * 1024 * 1024),
        name="update_panel",
    )(order, ranks, rows_l, rows_r, tile, rows_w, trailing, right_sides)


def on_device(n_row, n_col, trailing, panel_left, panel_right, panel_solved, right_sides, tile_ranks, tile_order):
    rows_l, rows_r, tile, rows_w = gather(n_row, n_col, tile_order, panel_left, panel_right, panel_solved)
    return update(tile_order, tile_ranks, rows_l, rows_r, tile, rows_w, trailing, right_sides)


def solution(mesh):
    return jax.shard_map(
        functools.partial(on_device, mesh.shape["row"], mesh.shape["col"]),
        mesh=mesh,
        in_specs=(
            P("row", "col"),
            P(("row", "col"), None),
            P("row", "col", None),
            P("row", "col"),
            P("row", "col"),
            P(),
            P(),
        ),
        out_specs=(P("row", "col"), P("row", "col")),
        check_vma=False,
    )
```

```python
import functools

import jax
import jax.numpy as jnp
from jax import lax
from jax.experimental import pallas as pl
from jax.experimental.pallas import tpu as pltpu
from jax.sharding import PartitionSpec as P

MESH = pl.DeviceIdType.MESH
ACROSS = 2
CORES = 2


def sides(z, length, d, body):
    for side in range(2):
        src = z - d if side == 0 else z + d
        ok = src >= 0 if side == 0 else (src < length) & (d > 0)
        pl.when(ok & (d >= 0))(functools.partial(body, src, side))


def find(order, value):
    place = jnp.int32(0)
    for i in range(order.shape[0]):
        place = jnp.where(order[i] == value, jnp.int32(i), place)
    return place


def gather_kernel(n_row, n_col, slots, order, left, right, solved, rows_l, both_out, tile,
                  rows_r, rows_w, first_out, first_in, chip, far_in, own_sem, rsem, zsem, ysem, fsem, frsem, xsem, xrsem, tsem, trsem, wsem, wrsem):
    length = n_col // ACROSS
    half = length // slots
    teams = n_row // CORES
    part = tile.shape[1] // CORES
    late = slots + 1
    row, col = lax.axis_index("row"), lax.axis_index("col")
    z, y = col // ACROSS, col % ACROSS
    team, core = row // CORES, row % CORES
    pair = team * CORES + (1 - core)
    mate = z * ACROSS + (1 - y)

    barrier = pltpu.get_barrier_semaphore()

    def greet(r, c):
        pl.semaphore_signal(barrier, inc=1, device_id=(r, c), device_id_type=MESH)

    @pl.when(z > 0)
    def _():
        greet(row, col - ACROSS)

    @pl.when(z < length - 1)
    def _():
        greet(row, col + ACROSS)

    greet(row, mate)
    for k in range(1, n_row):
        greet(lax.rem(row + k, n_row), col)

    cut = left.shape[0] // 2

    def piece(p, c):
        if p == 0:
            return rows_l.at[c, pl.ds(0, cut)]
        if p == late:
            return rows_l.at[c, pl.ds(cut, cut)]
        return rows_r.at[p - 1, c]

    own = [pltpu.make_async_copy(left, rows_l.at[col], own_sem.at[0])]
    for s in range(slots):
        own.append(pltpu.make_async_copy(right.at[s], piece(s + 1, col), own_sem.at[s + 1]))
    own.append(pltpu.make_async_copy(solved, rows_w.at[row], own_sem.at[slots + 1]))
    for copy in own:
        copy.start()
    for copy in own:
        copy.wait()
    pl.semaphore_wait(barrier, (z > 0).astype(jnp.int32) + (z < length - 1).astype(jnp.int32) + n_row)

    def z_copy(p, src, way, across=None):
        c = src * ACROSS + (y if across is None else across)
        lane = p if across is None else late + 1
        to = col + (ACROSS if way == 0 else -ACROSS)
        return pltpu.make_async_remote_copy(piece(p, c), piece(p, c), zsem.at[way, lane, src], rsem.at[p, c], device_id=(row, to), device_id_type=MESH)

    def y_copy(p, src, c):
        return pltpu.make_async_remote_copy(piece(p, c), piece(p, c), ysem.at[p, src], rsem.at[p, c], device_id=(row, mate), device_id_type=MESH)

    def w_copy(k):
        return pltpu.make_async_remote_copy(rows_w.at[row], rows_w.at[row], wsem.at[k], wrsem.at[row], device_id=(lax.rem(row + k, n_row), col), device_id_type=MESH)

    def f_copy(c):
        return pltpu.make_async_remote_copy(first_out.at[c], first_in.at[c], fsem.at[c], frsem.at[c], device_id=(pair, col), device_id_type=MESH)

    def x_copy(c, k, source):
        to = lax.rem(team + k, teams)
        return pltpu.make_async_remote_copy(chip.at[c], far_in.at[source, c], xsem.at[k, c], xrsem.at[source, c], device_id=(to * CORES + core, col), device_id_type=MESH)

    def rows_of(which):
        return pl.ds(pl.multiple_of(which * part, part), part)

    def t_copy(c, which):
        ref = tile.at[c, rows_of(which)]
        return pltpu.make_async_remote_copy(ref, ref, tsem.at[c], trsem.at[c], device_id=(pair, col), device_id_type=MESH)

    root_slot = find(order, col)
    local = lax.rem(root_slot, slots)
    root_row = root_slot // slots
    root_team = root_row // CORES

    def candidate(c, which, is_left):
        parts = []
        for s in range(slots):
            if is_left:
                parts.append(rows_l[(c - n_col) + s * (n_col // slots), rows_of(which)])
            else:
                parts.append(rows_r[s, c, rows_of(which)])
        value = parts[0]
        for s in range(1, slots):
            value = jnp.where(local == s, parts[s], value)
        return value

    def stage_one(c, is_left):
        first_out[c] = candidate(c, 1 - core, is_left)
        f_copy(c).start()

    def stage_two(c, is_left):
        mine = candidate(c, core, is_left)
        f_copy(c).wait_recv()
        chip[c] = jnp.where(root_row == row, mine, first_in[c])
        for k in range(1, teams):
            x_copy(c, k, team).start()

    def stage_three(c, is_left):
        value = chip[c]
        for k in range(1, teams):
            other = lax.rem(team + k, teams)
            x_copy(c, k, other).wait_recv()
            value = jnp.where(root_team == other, far_in[other, c], value)
        tile[c, rows_of(core)] = value
        t_copy(c, core).start()

    def sources(d, body):
        sides(z, length, d, body)

    def near(d, body):
        sources(d, lambda src, side: body(src * ACROSS + y, False))

    def lefts(d, body):
        def one(q, _):
            last = jnp.abs(z - q)
            for s in range(1, slots):
                last = jnp.maximum(last, jnp.abs(z - q - s * half))

            @pl.when(last == d)
            def _():
                for across in range(ACROSS):
                    body(n_col + q * ACROSS + across, True)

            return 0

        lax.fori_loop(0, half, one, 0)

    def far(d, body):
        sources(d, lambda src, side: body(src * ACROSS + 1 - y, False))

    def along(d, side, act):
        @pl.when((z < length - 1) & ((side == 0) | (d == 0)))
        def _():
            act(0)

        @pl.when((z > 0) & ((side == 1) | (d == 0)))
        def _():
            act(1)

    def pass_on(d, pieces):
        for p in pieces:
            def one(src, side, p=p):
                @pl.when(d > 0)
                def _():
                    y_copy(p, src, src * ACROSS + y).wait_recv()

                y_copy(p, src, src * ACROSS + y).start()
                along(d, side, lambda way: z_copy(p, src, way).start())

            sources(d, one)

    def pass_late(d):
        def both(src, side):
            @pl.when(d > 0)
            def _():
                y_copy(late, src, src * ACROSS + y).wait_recv()

            @pl.when(d == 0)
            def _():
                y_copy(late, src, src * ACROSS + y).start()

            along(d, side, lambda way: z_copy(late, src, way).start())
            y_copy(late, src, src * ACROSS + 1 - y).wait_recv()
            along(d, side, lambda way: z_copy(late, src, way, 1 - y).start())

        sources(d, both)

    def arrive(d, pieces):
        def one(src, side):
            for p in pieces:
                y_copy(p, src, src * ACROSS + 1 - y).wait_recv()

        sources(d, one)

    def w_wait():
        for k in range(1, n_row):
            w_copy(k).wait_send()
            other = lax.rem(row + k, n_row)
            ref = rows_w.at[other]
            pltpu.make_async_remote_copy(ref, ref, wsem.at[k], wrsem.at[other], device_id=(other, col), device_id_type=MESH).wait_recv()

    width = tile.shape[2]
    depth = tile.shape[1]
    per = n_col // n_row
    both_out[...] = jnp.zeros_like(both_out)

    def accumulate(t):
        def one(c, _):
            src = c // ACROSS
            when = jnp.abs(z - src) + 2

            @pl.when(when == t)
            def _():
                t_copy(c, 1 - core).wait_recv()
                start = pl.multiple_of((c % per) * depth, depth)
                others = cut_two(rows_w[c // per, pl.ds(start, depth)])
                column = cut_two(tile[c])
                for s in range(slots):
                    mine = cut_two(rows_r[s, c])
                    both_out[s, :, :width] += dot3(mine, column, ((0,), (0,)))
                    both_out[s, :, width:] += dot3(mine, others, ((0,), (0,)))

            return 0

        lax.fori_loop(0, n_col, one, 0)

    early = tuple(range(late))

    def step(t, _):
        pass_on(t, early)
        pass_late(t)
        near(t, stage_one)

        @pl.when(t == 0)
        def _():
            for k in range(1, n_row):
                w_copy(k).start()

        arrive(t - 1, early)
        lefts(t - 1, stage_one)
        far(t - 1, stage_one)
        near(t, stage_two)
        lefts(t - 1, stage_two)
        far(t - 1, stage_two)
        near(t - 1, stage_three)
        lefts(t - 2, stage_three)
        far(t - 2, stage_three)

        @pl.when(t == 2)
        def _():
            w_wait()

        accumulate(t)
        return 0

    lax.fori_loop(0, length + 2, step, 0)

    def drain(d, _):
        def one(src, side):
            for p in range(late):
                y_copy(p, src, src * ACROSS + y).wait_send()
                along(d, side, lambda way: z_copy(p, src, way).wait_send())

            @pl.when(d == 0)
            def _():
                y_copy(late, src, src * ACROSS + y).wait_send()

            along(d, side, lambda way: z_copy(late, src, way).wait_send())
            along(d, side, lambda way: z_copy(late, src, way, 1 - y).wait_send())

        sources(d, one)
        return 0

    lax.fori_loop(0, length, drain, 0)

    def finish(c, _):
        f_copy(c).wait_send()
        for k in range(1, teams):
            x_copy(c, k, team).wait_send()
        t_copy(c, core).wait_send()

        @pl.when(c >= n_col)
        def _():
            t_copy(c, 1 - core).wait_recv()

        return 0

    lax.fori_loop(0, n_col + half * ACROSS, finish, 0)


def gather(n_row, n_col, order, left, right, solved):
    slots, depth, width = right.shape
    length = n_col // ACROSS
    teams = n_row // CORES
    chunks = n_col + n_col // slots
    f32 = jnp.float32
    block = (depth, width)
    part = (depth // CORES, width)
    vmem = pl.BlockSpec(memory_space=pltpu.VMEM)
    hbm = pl.BlockSpec(memory_space=pltpu.HBM)
    dma = pltpu.SemaphoreType.DMA
    return pl.pallas_call(
        functools.partial(gather_kernel, n_row, n_col, slots),
        out_shape=(
            jax.ShapeDtypeStruct((n_col,) + left.shape, f32),
            jax.ShapeDtypeStruct((slots, width, width + solved.shape[1]), f32),
            jax.ShapeDtypeStruct((chunks,) + block, f32),
        ),
        in_specs=[pl.BlockSpec(memory_space=pltpu.SMEM), hbm, hbm, hbm],
        out_specs=(vmem, vmem, vmem),
        scratch_shapes=[
            pltpu.VMEM((slots, n_col) + block, f32),
            pltpu.VMEM((n_row,) + solved.shape, f32),
            pltpu.VMEM((chunks,) + part, f32),
            pltpu.VMEM((chunks,) + part, f32),
            pltpu.VMEM((chunks,) + part, f32),
            pltpu.VMEM((teams, chunks) + part, f32),
            dma((slots + 2,)),
            dma((slots + 2, n_col)),
            dma((2, slots + 3, length)),
            dma((slots + 2, length)),
            dma((chunks,)),
            dma((chunks,)),
            dma((teams, chunks)),
            dma((teams, chunks)),
            dma((chunks,)),
            dma((chunks,)),
            dma((n_row,)),
            dma((n_row,)),
        ],
        compiler_params=pltpu.CompilerParams(collective_id=0, has_side_effects=True, vmem_limit_bytes=55 * 1024 * 1024),
        name="gather_panel",
    )(order, left, right, solved)


def cut_two(x):
    high = x.astype(jnp.bfloat16)
    return high, (x - high.astype(jnp.float32)).astype(jnp.bfloat16)


def dot3(a, b, dims):
    (ah, al), (bh, bl) = a, b

    def dot(u, v):
        return lax.dot_general(u, v, (dims, ((), ())), preferred_element_type=jnp.float32)

    return dot(ah, bh) + (dot(ah, bl) + dot(al, bh))


def update_kernel(order, ranks, rows_l, both, tile, trailing, sides_in, trail_out, rhs_out, mid_high, mid_low):
    slots, width = both.shape[0], both.shape[1]
    slot, step = pl.program_id(0), pl.program_id(1)

    @pl.when(step == 0)
    def _():
        tile_id = order[lax.axis_index("row") * slots + slot]
        rank = ranks[tile_id]
        column_rank = ranks[lax.axis_index("col")]
        lane = lax.broadcasted_iota(jnp.int32, (1, width), 1)
        sub = lax.broadcasted_iota(jnp.int32, (width, 1), 0)
        tile_left = tile[...].reshape(-1, width)
        tile_left = cut_two(jnp.where(lane < column_rank, tile_left, 0.0))
        gram = cut_two(jnp.where(sub < rank, both[slot, :, :width], 0.0))
        middle = dot3(gram, tile_left, ((1,), (1,)))
        rows = middle.shape[1]
        mid_high[:, :rows], mid_low[:, :rows] = cut_two(middle)
        mid_high[:, rows:], mid_low[:, rows:] = cut_two(jnp.where(sub < rank, both[slot, :, width:], 0.0))

    left = cut_two(rows_l[0])
    update = dot3(left, (mid_high[...], mid_low[...]), ((1,), (0,)))
    rows = trailing.shape[1]
    trail_out[...] = trailing[...] - update[:, :rows]
    rhs_out[...] = sides_in[...] - update[:, rows:]


def update(order, ranks, rows_l, both, tile, trailing, right_sides):
    slots, width = both.shape[0], both.shape[1]
    rows, columns = trailing.shape
    others = right_sides.shape[1]
    blocks = 2
    size = rows // slots // blocks
    rows_l = rows_l.reshape(slots * blocks, size, width)
    chunks, depth = tile.shape[0], tile.shape[1]
    lefts = columns // depth
    smem = pl.BlockSpec(memory_space=pltpu.SMEM)
    vmem = pl.BlockSpec(memory_space=pltpu.VMEM)

    def place(s, i):
        return (s * blocks + i, 0)

    return pl.pallas_call(
        update_kernel,
        grid=(slots, blocks),
        out_shape=(jax.ShapeDtypeStruct(trailing.shape, jnp.float32), jax.ShapeDtypeStruct(right_sides.shape, jnp.float32)),
        in_specs=[
            smem,
            smem,
            pl.BlockSpec((1, size, width), lambda s, i: (s * blocks + i, 0, 0)),
            vmem,
            pl.BlockSpec((lefts, depth, width), lambda s, i: (chunks // lefts - 1, 0, 0)),
            pl.BlockSpec((size, columns), place),
            pl.BlockSpec((size, others), place),
        ],
        out_specs=(pl.BlockSpec((size, columns), place), pl.BlockSpec((size, others), place)),
        scratch_shapes=[pltpu.VMEM((width, columns + others), jnp.bfloat16)] * 2,
        compiler_params=pltpu.CompilerParams(vmem_limit_bytes=55 * 1024 * 1024),
        name="update_panel",
    )(order, ranks, rows_l, both, tile, trailing, right_sides)


def on_device(n_row, n_col, trailing, panel_left, panel_right, panel_solved, right_sides, tile_ranks, tile_order):
    rows_l, both, tile = gather(n_row, n_col, tile_order, panel_left, panel_right, panel_solved)
    return update(tile_order, tile_ranks, rows_l, both, tile, trailing, right_sides)


def solution(mesh):
    return jax.shard_map(
        functools.partial(on_device, mesh.shape["row"], mesh.shape["col"]),
        mesh=mesh,
        in_specs=(
            P("row", "col"),
            P(("row", "col"), None),
            P("row", "col", None),
            P("row", "col"),
            P("row", "col"),
            P(),
            P(),
        ),
        out_specs=(P("row", "col"), P("row", "col")),
        check_vma=False,
    )
```
